256 devices in a mesh: island: 8 (over y_lo, x), fsdp: 32 (over z, y_hi, core).
Axes of the slice: x: 4, y: 4 (y_hi: 2, y_lo: 2; y = y_hi * 2 + y_lo), z: 8, core: 2. Of those that a mesh axis runs over, the one named last changes fastest.
Arguments:
- global_params: bfloat16 [8, 1, 4096, 8192], P('island', None, 'fsdp'), may hold values from -6 to 6
- local_params: bfloat16 [8, 1, 4096, 8192], P('island', None, 'fsdp'), may hold values from -6 to 6
- momentum: bfloat16 [8, 1, 4096, 8192], P('island', None, 'fsdp'), may hold values from -6 to 6
- init_factors: float32 [4, 1, 4, 8192], replicated, may hold values from -6 to 6
- seeds: int32 [8], replicated, may hold values from 0 to 3, as said below
- plan: int32 [8], replicated, may hold values from 1 to 4, as said below
- round_index: int32 [], replicated, may hold values from 0 to 999
Outputs:
- new_params: bfloat16 [8, 1, 4096, 8192], P('island', None, 'fsdp')
- new_momentum: bfloat16 [8, 1, 4096, 8192], P('island', None, 'fsdp')
- warm_factors: float32 [8, 1, 4, 8192], P('island')
The draws below stay inside these ranges and needn't reach their ends.
Inputs may be any that keep to these rules, and one draw needn't show every extreme that they name: `plan`: every entry is a power of two; every power of two up to 4 appears. `seeds`: every value from 0 to 3 is used by some replica.
All inputs are finite; a program needn't handle non-finite values.
Results may differ from the reference program's by a relative error of at most 0.0017.
Values sent between devices are 32-bit elements; how exact they have to be, the bound alone decides.
No kernel may reach another device: no remote copies, remote signals or barrier semaphores. Data moves between devices by JAX's collectives and lax.ppermute only.
A program may use at most 64 MiB of HBM per device.

```python
import math
import jax
import jax.numpy as jnp
from jax import lax

COLS = 8192
ROWS = 4096
MATS = 1
RANK = 4
ITERS = 3
NSEED = 4
ROUNDS = 8
ISL = 8
N_ISLAND = 8


def draw_plan(key, part):
    levels = int(math.log2(N_ISLAND))
    covered = jax.random.permutation(jax.random.fold_in(key, 17), levels).astype(jnp.int32)
    others = jax.random.randint(jax.random.fold_in(key, 23), (ROUNDS - levels,), 0, levels).astype(jnp.int32)
    powers = jnp.concatenate([covered, others]).astype(jnp.int32)
    return jnp.left_shift(jnp.int32(1), powers).astype(jnp.int32)


def draw_seeds(key, part):
    order = jax.random.permutation(jax.random.fold_in(key, 29), ISL).astype(jnp.int32)
    return jnp.mod(order, NSEED).astype(jnp.int32)


def shard_levels(own_key, dims, shards, smallest, high):
    def one(position, blocks):
        heights = jax.random.uniform(jax.random.fold_in(jax.random.fold_in(own_key, 6), position), (blocks,), jnp.float32, smallest / len(shards), high / len(shards))
        return jnp.repeat(jnp.exp(heights), dims[position] // blocks).reshape((-1,) + (1,) * (len(dims) - position - 1))

    factor_of = one(*shards[0])
    for cut in shards[1:]:
        factor_of = factor_of * one(*cut)
    return factor_of


def centred(rng, dims, scale, reach, shards=(), held_as=jnp.bfloat16):
    drawn = scale * jax.random.normal(rng, dims, jnp.float32)
    if shards:
        drawn = drawn * shard_levels(rng, dims, shards, -0.22, 0.18)
    return jnp.clip(drawn, -reach, reach).astype(held_as)


def setup_inputs(seed: int = 0) -> dict:
    key_of = jax.random.split(jax.random.key(seed), 8)
    global_params = centred(key_of[0], (ISL, MATS, ROWS, COLS), 1.0, 6.0, ((0, 8), (2, 32)))
    local_params = centred(key_of[1], (ISL, MATS, ROWS, COLS), 1.0, 6.0, ((0, 8), (2, 32)))
    momentum = centred(key_of[2], (ISL, MATS, ROWS, COLS), 1.0, 6.0, ((0, 8), (2, 32)))
    init_factors = centred(key_of[3], (NSEED, MATS, RANK, COLS), 1.0, 6.0, (), jnp.float32)
    seeds = draw_seeds(jax.random.fold_in(key_of[7], 71), 0)
    plan = draw_plan(jax.random.fold_in(key_of[7], 71), 0)
    round_index = jax.random.randint(key_of[6], (), 0, 1000).astype(jnp.int32)
    return {"global_params": global_params, "local_params": local_params, "momentum": momentum, "init_factors": init_factors, "seeds": seeds, "plan": plan, "round_index": round_index}


def reference(global_params, local_params, momentum, init_factors, seeds, plan, round_index):
    high = lax.Precision.HIGHEST
    offset = plan[jnp.mod(round_index, plan.shape[0])]

    def one_replica(island_pos):
        partner = jnp.bitwise_xor(island_pos, offset).astype(jnp.int32)
        start = global_params[island_pos].astype(jnp.float32)
        delta = start - local_params[island_pos].astype(jnp.float32)
        other = global_params[partner].astype(jnp.float32) - local_params[partner].astype(jnp.float32)
        diff = delta - other
        factor = init_factors[seeds[jnp.minimum(island_pos, partner)]]
        basis = None
        for turn in range(ITERS):
            left = jnp.einsum('mkc,mrc->mkr', factor, diff, precision=high)
            gram = jnp.einsum('mkr,mjr->mkj', left, left, precision=high)
            lower = jnp.linalg.cholesky(gram)
            basis = lax.linalg.triangular_solve(lower, left, left_side=True, lower=True)
            factor = jnp.einsum('mkr,mrc->mkc', basis, diff, precision=high)
        correction = jnp.einsum('mkr,mkc->mrc', basis, factor, precision=high)
        gossiped = delta - 0.5 * correction
        velocity = 0.9 * momentum[island_pos].astype(jnp.float32) + gossiped
        updated = start - 0.7 * (gossiped + 0.9 * velocity)
        return (updated.astype(jnp.bfloat16), velocity.astype(jnp.bfloat16), factor)
    return lax.map(one_replica, jnp.arange(N_ISLAND, dtype=jnp.int32))
```

```python
import jax
import jax.numpy as jnp
from jax import lax
from jax.sharding import PartitionSpec as P

ITERS = 3
HIGH = lax.Precision.HIGHEST


def exchanged(x, level, fsdp_mask, island_mask):
    both = ("island", "fsdp")
    n_island, n_fsdp = lax.axis_size("island"), lax.axis_size("fsdp")
    if island_mask == 0:
        return lax.ppermute(x, "fsdp", [(i, i ^ fsdp_mask) for i in range(n_fsdp)])
    if fsdp_mask == 0:
        return lax.ppermute(x, "island", [(i, i ^ island_mask) for i in range(n_island)])
    pairs = []
    for i in range(n_island):
        for f in range(n_fsdp):
            pairs.append((i * n_fsdp + f, (i ^ island_mask) * n_fsdp + (f ^ fsdp_mask)))
    return lax.ppermute(x, both, pairs)


def summed(part, level, core):
    rank, cols = part.shape
    halves = part.reshape(rank, 2, cols // 2)
    keep = lax.dynamic_index_in_dim(halves, core, 1, keepdims=False)
    give = lax.dynamic_index_in_dim(halves, 1 - core, 1, keepdims=False)
    total = keep + exchanged(give, level, 1, 0)
    for mask in (4, 8, 24):
        total = total + exchanged(total, level, mask, 0)
    total = total + exchanged(total, level, 0, 1 << level)
    if level == 2:
        total = total + exchanged(total, level, 2, 4)
    else:
        total = total + exchanged(total, level, 2, 0)
    other = exchanged(total, level, 1, 0)
    first = jnp.where(core == 0, total, other)
    second = jnp.where(core == 0, other, total)
    return jnp.concatenate([first, second], axis=1)


def make_branch(level):

    def run(factor, delta):
        core = lax.axis_index("fsdp") % 2
        left = basis = None
        for turn in range(ITERS):
            mine_left = jnp.einsum("kc,rc->kr", factor, delta, precision=HIGH)
            left = mine_left - exchanged(mine_left, level, 0, 1 << level)
            part = jnp.einsum("kr,rc->kc", left, delta, precision=HIGH)
            right = summed(part, level, core)
            gram = jnp.einsum("kc,jc->kj", factor, right, precision=HIGH)
            lower = jnp.linalg.cholesky(gram, symmetrize_input=False)
            eye = jnp.eye(lower.shape[0], dtype=lower.dtype)
            inverse = lax.linalg.triangular_solve(lower, eye, left_side=True, lower=True)
            factor = jnp.einsum("kj,jc->kc", inverse, right, precision=HIGH)
            basis = jnp.einsum("kj,jr->kr", inverse, left, precision=HIGH)
        return basis, factor

    return run


def on_device(global_params, local_params, momentum, init_factors, seeds, plan, round_index):
    offset = plan[jnp.mod(round_index, plan.shape[0])]
    island_pos = lax.axis_index("island")
    partner = jnp.bitwise_xor(island_pos, offset)
    factor = init_factors[seeds[jnp.minimum(island_pos, partner)], 0]
    start = global_params[0, 0].astype(jnp.float32)
    delta = start - local_params[0, 0].astype(jnp.float32)
    which_bit = offset // 2
    basis, factor = lax.switch(which_bit, [make_branch(level) for level in range(3)], factor, delta)
    correction = jnp.einsum("kr,kc->rc", basis, factor, precision=HIGH)
    gossiped = delta - 0.5 * correction
    velocity = 0.9 * momentum[0, 0].astype(jnp.float32) + gossiped
    updated = start - 0.7 * (gossiped + 0.9 * velocity)
    return (updated.astype(jnp.bfloat16)[None, None], velocity.astype(jnp.bfloat16)[None, None], factor[None, None])


def solution(mesh):
    return jax.shard_map(
        on_device,
        mesh=mesh,
        in_specs=(
            P("island", None, "fsdp", None),
            P("island", None, "fsdp", None),
            P("island", None, "fsdp", None),
            P(),
            P(),
            P(),
            P(),
        ),
        out_specs=(
            P("island", None, "fsdp", None),
            P("island", None, "fsdp", None),
            P("island", None, None, None),
        ),
        check_vma=False,
    )
```

```python
import functools

import jax
import jax.numpy as jnp
from jax import lax
from jax.experimental import pallas as pl
from jax.experimental.pallas import tpu as pltpu
from jax.sharding import PartitionSpec as P

ITERS = 3
F32 = jnp.float32
BF16 = jnp.bfloat16
VMEM = pl.BlockSpec(memory_space=pltpu.VMEM)
SMEM = pl.BlockSpec(memory_space=pltpu.SMEM)
ANY = pl.BlockSpec(memory_space=pl.ANY)
CHUNK = 512
LIMIT = 24 << 20


def split3(x):
    high = x.astype(BF16).astype(F32)
    rest = x - high
    middle = rest.astype(BF16).astype(F32)
    return high, middle, rest - middle


def stacked(x):
    return jnp.concatenate(split3(x), axis=0).astype(BF16)


def unstacked(x):
    rank = x.shape[0] // 3
    return x[0:rank] + x[rank : 2 * rank] + x[2 * rank : 3 * rank]


def columns(start, width):
    return pl.ds(pl.multiple_of(start, width), width)


def left_product(factor, both):
    return lax.dot_general(stacked(factor), both, (((1,), (1,)), ((), ())), preferred_element_type=F32)


def folded(acc):
    rows = acc.shape[1] // 2
    total = unstacked(acc)
    return total[:, :rows] + total[:, rows:]


def first_kernel(seeds, plan, turn, init, start, local, level, factor, both, left, sem):
    offset = plan[lax.rem(turn[0], plan.shape[0])]
    island = lax.axis_index("island")
    chosen = seeds[jnp.minimum(island, jnp.bitwise_xor(island, offset))]
    fetch = pltpu.make_async_copy(init.at[chosen, 0], factor, sem)
    fetch.start()
    level[0] = lax.shift_right_logical(offset, 1)
    rows, cols = start.shape

    def split(j, carry):
        s = columns(j * CHUNK, CHUNK)
        delta = start[:, s].astype(F32) - local[:, s].astype(F32)
        high = delta.astype(BF16)
        both[0:rows, s] = high
        both[rows : 2 * rows, s] = (delta - high.astype(F32)).astype(BF16)
        return carry

    lax.fori_loop(0, cols // CHUNK, split, 0)
    fetch.wait()
    rank = factor.shape[0]

    def product(j, acc):
        s = columns(j * CHUNK, CHUNK)
        return acc + left_product(factor[:, s], both[:, s])

    left[...] = folded(lax.fori_loop(0, cols // CHUNK, product, jnp.zeros((3 * rank, 2 * rows), F32)))


def right_kernel(mine, peer, both, left, keep, give):
    core = lax.rem(lax.axis_index("fsdp"), 2)
    diff = mine[...] - peer[...]
    left[...] = diff
    lhs = stacked(diff)
    lhs = jnp.concatenate([lhs, lhs], axis=1)
    half = keep.shape[1]

    def step(j, carry):
        s = columns(j * CHUNK, CHUNK)
        for out, side in ((give, 1 - core), (keep, core)):
            t = columns(side * half + j * CHUNK, CHUNK)
            out[:, s] = unstacked(jnp.dot(lhs, both[:, t], preferred_element_type=F32))
        return carry

    lax.fori_loop(0, half // CHUNK, step, 0)


def inverse_factor(old, own, other, core):
    rank, half = own.shape

    def step(j, accs):
        s = columns(j * CHUNK, CHUNK)
        for part, side in ((own, core), (other, 1 - core)):
            t = columns(side * half + j * CHUNK, CHUNK)
            q = old[:, t]
            u = part[:, s]
            accs = tuple(acc + q * u[k : k + 1, :] for k, acc in enumerate(accs))
        return accs

    zero = jnp.zeros((rank, CHUNK), F32)
    accs = lax.fori_loop(0, half // CHUNK, step, (zero,) * rank)
    gram = [jnp.sum(acc, axis=1, keepdims=True) for acc in accs]
    g = [[gram[j][i : i + 1, :] for j in range(rank)] for i in range(rank)]
    lower = [[None] * rank for _ in range(rank)]
    inv = [[None] * rank for _ in range(rank)]
    for j in range(rank):
        d = g[j][j]
        for k in range(j):
            d = d - lower[j][k] * lower[j][k]
        root = jnp.sqrt(d)
        inv[j][j] = 1.0 / root
        for i in range(j + 1, rank):
            s = g[i][j]
            for k in range(j):
                s = s - lower[i][k] * lower[j][k]
            lower[i][j] = s * inv[j][j]
    for j in range(rank):
        for i in range(j + 1, rank):
            s = lower[i][j] * inv[j][j]
            for k in range(j + 1, i):
                s = s + lower[i][k] * inv[k][j]
            inv[i][j] = -s * inv[i][i]
    row = lax.broadcasted_iota(jnp.int32, (rank, 1), 0)
    cols = []
    for j in range(rank):
        col = jnp.zeros((rank, 1), F32)
        for i in range(j, rank):
            col = jnp.where(row == i, inv[i][j], col)
        cols.append(col)
    return cols


def solved(cols, u):
    total = cols[0] * u[0:1, :]
    for k in range(1, len(cols)):
        total = total + cols[k] * u[k : k + 1, :]
    return total


def middle_kernel(old, own, other, both, factor, left):
    core = lax.rem(lax.axis_index("fsdp"), 2)
    rank, half = own.shape
    inv = inverse_factor(old, own, other, core)

    def step(j, acc):
        s = columns(j * CHUNK, CHUNK)
        for part, side in ((own, core), (other, 1 - core)):
            t = columns(side * half + j * CHUNK, CHUNK)
            q = solved(inv, part[:, s])
            factor[:, t] = q
            acc = acc + left_product(q, both[:, t])
        return acc

    left[...] = folded(lax.fori_loop(0, half // CHUNK, step, jnp.zeros((3 * rank, both.shape[0]), F32)))


def last_kernel(old, own, other, left, start, local, momentum, params_hbm, momentum_hbm, factor_hbm, params, moved, factor, sems, factor_sem):
    core = lax.rem(lax.axis_index("fsdp"), 2)
    rank, half = own.shape
    inv = inverse_factor(old, own, other, core)
    b1, b2, b3 = split3(solved(inv, left[...]))
    basis = jnp.concatenate([b1, b1, b2, b2, b1, b3], axis=0).T.astype(BF16)

    def step(j, carry):
        s = columns(j * CHUNK, CHUNK)
        for n, (part, side) in enumerate(((own, core), (other, 1 - core))):
            t = columns(side * half + j * CHUNK, CHUNK)
            q = solved(inv, part[:, s])
            factor[:, t] = q
            q1, q2, q3 = split3(q)
            rhs = jnp.concatenate([q1, q2, q1, q2, q3, q1], axis=0).astype(BF16)
            correction = jnp.dot(basis, rhs, preferred_element_type=F32)
            base = start[:, t].astype(F32)
            gossiped = (base - local[:, t].astype(F32)) - 0.5 * correction
            velocity = 0.9 * momentum[:, t].astype(F32) + gossiped
            moved[:, t] = velocity.astype(BF16)
            params[:, t] = (base - 0.7 * (gossiped + 0.9 * velocity)).astype(BF16)
            pltpu.make_async_copy(moved.at[:, t], momentum_hbm.at[:, t], sems.at[0, n, j]).start()
            pltpu.make_async_copy(params.at[:, t], params_hbm.at[:, t], sems.at[1, n, j]).start()
        return carry

    lax.fori_loop(0, half // CHUNK, step, 0)
    sent = pltpu.make_async_copy(factor, factor_hbm, factor_sem)
    sent.start()

    def drain(j, carry):
        for n, side in enumerate((core, 1 - core)):
            t = columns(side * half + j * CHUNK, CHUNK)
            pltpu.make_async_copy(moved.at[:, t], momentum_hbm.at[:, t], sems.at[0, n, j]).wait()
            pltpu.make_async_copy(params.at[:, t], params_hbm.at[:, t], sems.at[1, n, j]).wait()
        return carry

    lax.fori_loop(0, half // CHUNK, drain, 0)
    sent.wait()


def exchanged(x, fsdp_mask, island_mask):
    n_island, n_fsdp = lax.axis_size("island"), lax.axis_size("fsdp")
    if island_mask == 0:
        return lax.ppermute(x, "fsdp", [(i, i ^ fsdp_mask) for i in range(n_fsdp)])
    if fsdp_mask == 0:
        return lax.ppermute(x, "island", [(i, i ^ island_mask) for i in range(n_island)])
    pairs = []
    for i in range(n_island):
        for f in range(n_fsdp):
            pairs.append((i * n_fsdp + f, (i ^ island_mask) * n_fsdp + (f ^ fsdp_mask)))
    return lax.ppermute(x, ("island", "fsdp"), pairs)


def peer_left(k, x):
    return exchanged(x, 0, 1 << k)


def peer_sum(k, total):
    total = total + exchanged(total, 0, 1 << k)
    return total + exchanged(total, 2, 4 if k == 2 else 0)


def on_device(global_params, local_params, momentum, init_factors, seeds, plan, round_index):
    start, local, moment = global_params[0, 0], local_params[0, 0], momentum[0, 0]
    rows, cols = start.shape
    rank = init_factors.shape[2]
    half = cols // 2
    params = pltpu.CompilerParams(vmem_limit_bytes=LIMIT)
    wide = jax.ShapeDtypeStruct((rank, cols), F32)
    narrow = jax.ShapeDtypeStruct((rank, half), F32)
    small = jax.ShapeDtypeStruct((rank, rows), F32)
    pieces = jax.ShapeDtypeStruct((2 * rows, cols), BF16)
    level, factor, both, mine = pl.pallas_call(
        first_kernel,
        out_shape=(jax.ShapeDtypeStruct((1,), jnp.int32), wide, pieces, small),
        in_specs=[SMEM, SMEM, SMEM, ANY, VMEM, VMEM],
        out_specs=(SMEM, VMEM, VMEM, VMEM),
        scratch_shapes=[pltpu.SemaphoreType.DMA],
        compiler_params=params,
        name="first",
    )(seeds, plan, round_index.reshape(1), init_factors, start, local)
    which = level[0]
    for turn in range(ITERS):
        peer = lax.switch(which, [functools.partial(peer_left, k) for k in range(3)], mine)
        left, keep, give = pl.pallas_call(
            right_kernel,
            out_shape=(small, narrow, narrow),
            in_specs=[VMEM] * 3,
            out_specs=(VMEM,) * 3,
            compiler_params=params,
            name="right",
        )(mine, peer, both)
        total = keep + exchanged(give, 1, 0)
        for mask in (4, 8, 24):
            total = total + exchanged(total, mask, 0)
        total = lax.switch(which, [functools.partial(peer_sum, k) for k in range(3)], total)
        other = exchanged(total, 1, 0)
        if turn < ITERS - 1:
            factor, mine = pl.pallas_call(
                middle_kernel,
                out_shape=(wide, small),
                in_specs=[VMEM] * 4,
                out_specs=(VMEM,) * 2,
                compiler_params=params,
                name="middle",
            )(factor, total, other, both)
    big = jax.ShapeDtypeStruct((rows, cols), BF16)
    new_params, new_momentum, warm = pl.pallas_call(
        last_kernel,
        out_shape=(big, big, wide),
        in_specs=[VMEM] * 7,
        out_specs=(ANY,) * 3,
        scratch_shapes=[
            pltpu.VMEM((rows, cols), BF16),
            pltpu.VMEM((rows, cols), BF16),
            pltpu.VMEM((rank, cols), F32),
            pltpu.SemaphoreType.DMA((2, 2, half // CHUNK)),
            pltpu.SemaphoreType.DMA,
        ],
        compiler_params=params,
        name="last",
    )(factor, total, other, left, start, local, moment)
    return new_params[None, None], new_momentum[None, None], warm[None, None]


def solution(mesh):
    return jax.shard_map(
        on_device,
        mesh=mesh,
        in_specs=(
            P("island", None, "fsdp", None),
            P("island", None, "fsdp", None),
            P("island", None, "fsdp", None),
            P(),
            P(),
            P(),
            P(),
        ),
        out_specs=(
            P("island", None, "fsdp", None),
            P("island", None, "fsdp", None),
            P("island", None, None, None),
        ),
        check_vma=False,
    )
```

```python
import functools

import jax
import jax.numpy as jnp
from jax import lax
from jax.experimental import pallas as pl
from jax.experimental.pallas import tpu as pltpu
from jax.sharding import PartitionSpec as P

ITERS = 3
F32 = jnp.float32
BF16 = jnp.bfloat16
VMEM = pl.BlockSpec(memory_space=pltpu.VMEM)
SMEM = pl.BlockSpec(memory_space=pltpu.SMEM)
HBM = pl.BlockSpec(memory_space=pltpu.HBM)
ANY = pl.BlockSpec(memory_space=pl.ANY)
CHUNK = 512
PART = 1024
LANES = 128
LIMIT = 24 << 20


def split3(x):
    high = x.astype(BF16).astype(F32)
    rest = x - high
    middle = rest.astype(BF16).astype(F32)
    return high, middle, rest - middle


def stacked(x):
    return jnp.concatenate(split3(x), axis=0).astype(BF16)


def unstacked(x):
    rank = x.shape[0] // 3
    return x[0:rank] + x[rank : 2 * rank] + x[2 * rank : 3 * rank]


def columns(start, width):
    return pl.ds(pl.multiple_of(start, width), width)


def left_product(factor, both):
    return lax.dot_general(stacked(factor), both, (((1,), (1,)), ((), ())), preferred_element_type=F32)


def folded(acc):
    rows = acc.shape[1] // 2
    total = unstacked(acc)
    return total[:, :rows] + total[:, rows:]


def core_side(flip):
    core = lax.rem(lax.axis_index("fsdp"), 2)
    return 1 - core if flip else core


def split_kernel(start_hbm, local_hbm, both, start, local, sems):
    rows, cols = start.shape
    parts = cols // PART

    def loads(j, s):
        return (
            pltpu.make_async_copy(start_hbm.at[:, s], start.at[:, s], sems.at[0, j]),
            pltpu.make_async_copy(local_hbm.at[:, s], local.at[:, s], sems.at[1, j]),
        )

    for j in range(parts):
        for copy in loads(j, pl.ds(j * PART, PART)):
            copy.start()

    def step(j, carry):
        s = columns(j * PART, PART)
        for copy in loads(j, s):
            copy.wait()
        delta = start[:, s].astype(F32) - local[:, s].astype(F32)
        high = delta.astype(BF16)
        both[0:rows, s] = high
        both[rows : 2 * rows, s] = (delta - high.astype(F32)).astype(BF16)
        return carry

    lax.fori_loop(0, parts, step, 0)


def first_kernel(seeds, plan, turn, init, both, level, own, other, left):
    offset = plan[lax.rem(turn[0], plan.shape[0])]
    island = lax.axis_index("island")
    chosen = seeds[jnp.minimum(island, jnp.bitwise_xor(island, offset))]
    level[0] = lax.shift_right_logical(offset, 1)
    rank, half = own.shape
    own[...] = init[chosen, 0, :, columns(core_side(False) * half, half)]
    other[...] = init[chosen, 0, :, columns(core_side(True) * half, half)]

    def step(j, acc):
        s = columns(j * CHUNK, CHUNK)
        return acc + left_product(init[chosen, 0, :, s], both[:, s])

    acc = jnp.zeros((3 * rank, both.shape[0]), F32)
    left[...] = folded(lax.fori_loop(0, 2 * half // CHUNK, step, acc, unroll=2))


def difference(scale, mine, peer):
    diff = mine[...] - peer[...]
    if scale is None:
        return diff
    total = scale[0] * diff[0:1, :]
    for k in range(1, diff.shape[0]):
        total = total + scale[k] * diff[k : k + 1, :]
    return total


def right_half(left, both, out, side):
    lhs = stacked(left)
    lhs = jnp.concatenate([lhs, lhs], axis=1)
    half = out.shape[1]

    def step(j, carry):
        s = columns(j * CHUNK, CHUNK)
        t = columns(side * half + j * CHUNK, CHUNK)
        out[:, s] = unstacked(jnp.dot(lhs, both[:, t], preferred_element_type=F32))
        return carry

    lax.fori_loop(0, half // CHUNK, step, 0, unroll=2)


def give_kernel(*refs):
    scale = refs[0] if len(refs) == 6 else None
    mine, peer, both, give, left = refs[-5:]
    left[...] = difference(scale, mine, peer)
    right_half(left[...], both, give, core_side(True))


def keep_kernel(left, both, keep):
    right_half(left[...], both, keep, core_side(False))


def pair_sums(old, new):
    rank, half = new.shape

    def step(j, accs):
        s = columns(j * CHUNK, CHUNK)
        q = old[:, s]
        u = new[:, s]
        return tuple(acc + q * u[k : k + 1, :] for k, acc in enumerate(accs))

    accs = lax.fori_loop(0, half // CHUNK, step, (jnp.zeros((rank, CHUNK), F32),) * rank)
    out = []
    for acc in accs:
        total = acc[:, 0:LANES]
        for n in range(1, CHUNK // LANES):
            total = total + acc[:, n * LANES : (n + 1) * LANES]
        out.append(total)
    return out


def own_kernel(old, new, both, sums, product):
    rank, half = new.shape
    side = core_side(False)
    for k, total in enumerate(pair_sums(old, new)):
        sums[k] = total

    def step(j, acc):
        s = columns(j * CHUNK, CHUNK)
        t = columns(side * half + j * CHUNK, CHUNK)
        return acc + left_product(new[:, s], both[:, t])

    product[...] = folded(lax.fori_loop(0, half // CHUNK, step, jnp.zeros((3 * rank, both.shape[0]), F32), unroll=2))


def other_kernel(old, new, own_sums, own_product, both, sums, product):
    rank, half = new.shape
    side = core_side(True)
    for k, total in enumerate(pair_sums(old, new)):
        sums[k] = own_sums[k] + total

    def step(j, acc):
        s = columns(j * CHUNK, CHUNK)
        t = columns(side * half + j * CHUNK, CHUNK)
        return acc + left_product(new[:, s], both[:, t])

    acc = lax.fori_loop(0, half // CHUNK, step, jnp.zeros((3 * rank, both.shape[0]), F32), unroll=2)
    product[...] = own_product[...] + folded(acc)


def inverse_columns(scale, sums):
    rank = len(sums)
    gram = []
    for j in range(rank):
        dots = jnp.sum(sums[j], axis=1, keepdims=True) + jnp.zeros((rank, LANES), F32)
        if scale is not None:
            total = scale[0] * dots[0:1, :]
            for k in range(1, rank):
                total = total + scale[k] * dots[k : k + 1, :]
            dots = total
        gram.append(dots)
    g = [[gram[j][i : i + 1, :] for j in range(rank)] for i in range(rank)]
    lower = [[None] * rank for _ in range(rank)]
    inv = [[None] * rank for _ in range(rank)]
    for j in range(rank):
        d = g[j][j]
        for k in range(j):
            d = d - lower[j][k] * lower[j][k]
        inv[j][j] = 1.0 / jnp.sqrt(d)
        for i in range(j + 1, rank):
            s = g[i][j]
            for k in range(j):
                s = s - lower[i][k] * lower[j][k]
            lower[i][j] = s * inv[j][j]
    for j in range(rank):
        for i in range(j + 1, rank):
            s = lower[i][j] * inv[j][j]
            for k in range(j + 1, i):
                s = s + lower[i][k] * inv[k][j]
            inv[i][j] = -s * inv[i][i]
    row = lax.broadcasted_iota(jnp.int32, (rank, LANES), 0)
    cols = []
    for j in range(rank):
        col = jnp.zeros((rank, LANES), F32)
        for i in range(j, rank):
            col = jnp.where(row == i, inv[i][j], col)
        cols.append(col)
    return cols


def scale_kernel(*refs):
    *before, sums, out = refs
    scale = before[0] if before else None
    for k, col in enumerate(inverse_columns(scale, [sums[k] for k in range(sums.shape[0])])):
        out[k] = col


def last_kernel(scale, old_own, old_other, own, other, left, start, local, momentum, params_hbm, moved_hbm, factor_hbm, params, moved, factor, sems, factor_sem):
    rank, half = own.shape
    parts = half // CHUNK
    sides = (core_side(False), core_side(True))
    sums = [a + b for a, b in zip(pair_sums(old_own, own), pair_sums(old_other, other))]
    inv = inverse_columns(scale, sums)
    wide = [jnp.concatenate([col] * (CHUNK // LANES), axis=1) for col in inv]

    def solved(by, u):
        total = by[0] * u[0:1, :]
        for k in range(1, rank):
            total = total + by[k] * u[k : k + 1, :]
        return total

    def sends(j, n, t):
        return (
            pltpu.make_async_copy(moved.at[:, t], moved_hbm.at[0, 0, :, t], sems.at[0, n, j]),
            pltpu.make_async_copy(params.at[:, t], params_hbm.at[0, 0, :, t], sems.at[1, n, j]),
        )

    b1, b2, b3 = split3(solved(inv, left[...]))
    basis = jnp.concatenate([b1, b1, b2, b2, b1, b3], axis=0).T.astype(BF16)

    def step(j, carry):
        s = columns(j * CHUNK, CHUNK)
        for n, (part, side) in enumerate(zip((own, other), sides)):
            t = columns(side * half + j * CHUNK, CHUNK)
            q = solved(wide, part[:, s])
            factor[:, t] = q
            q1, q2, q3 = split3(q)
            rhs = jnp.concatenate([q1, q2, q1, q2, q3, q1], axis=0).astype(BF16)
            correction = jnp.dot(basis, rhs, preferred_element_type=F32)
            base = start[:, t].astype(F32)
            gossiped = (base - local[:, t].astype(F32)) - 0.5 * correction
            velocity = 0.9 * momentum[:, t].astype(F32) + gossiped
            moved[:, t] = velocity.astype(BF16)
            params[:, t] = (base - 0.7 * (gossiped + 0.9 * velocity)).astype(BF16)
            for copy in sends(j, n, t):
                copy.start()
        return carry

    lax.fori_loop(0, parts, step, 0)
    sent = pltpu.make_async_copy(factor, factor_hbm.at[0, 0], factor_sem)
    sent.start()

    def drain(j, carry):
        for n, side in enumerate(sides):
            for copy in sends(j, n, columns(side * half + j * CHUNK, CHUNK)):
                copy.wait()
        return carry

    lax.fori_loop(0, parts, drain, 0)
    sent.wait()


def exchanged(x, fsdp_mask, island_mask):
    n_island, n_fsdp = lax.axis_size("island"), lax.axis_size("fsdp")
    if island_mask == 0:
        return lax.ppermute(x, "fsdp", [(i, i ^ fsdp_mask) for i in range(n_fsdp)])
    if fsdp_mask == 0:
        return lax.ppermute(x, "island", [(i, i ^ island_mask) for i in range(n_island)])
    pairs = []
    for i in range(n_island):
        for f in range(n_fsdp):
            pairs.append((i * n_fsdp + f, (i ^ island_mask) * n_fsdp + (f ^ fsdp_mask)))
    return lax.ppermute(x, ("island", "fsdp"), pairs)


def local_call(kernel, name, inputs, out_shape, cost=(1 << 20, 1 << 20)):
    return pl.pallas_call(
        kernel,
        out_shape=out_shape,
        in_specs=[VMEM] * len(inputs),
        out_specs=jax.tree.map(lambda _: VMEM, out_shape),
        compiler_params=pltpu.CompilerParams(vmem_limit_bytes=LIMIT),
        cost_estimate=pl.CostEstimate(flops=cost[0], bytes_accessed=cost[1], transcendentals=0),
        name=name,
    )(*inputs)


def branch(k, own, other, both, mine, start, local, moment):
    rows, cols = start.shape
    rank, half = own.shape
    narrow = jax.ShapeDtypeStruct((rank, half), F32)
    small = jax.ShapeDtypeStruct((rank, rows), F32)
    square = jax.ShapeDtypeStruct((rank, rank, LANES), F32)
    scale = ()
    for turn in range(ITERS):
        peer = exchanged(mine, 0, 1 << k)
        give, left = local_call(give_kernel, "give", (*scale, mine, peer, both), (narrow, small))
        total = local_call(keep_kernel, "keep", (left, both), narrow) + exchanged(give, 1, 0)
        for mask in (4, 8, 24):
            total = total + exchanged(total, mask, 0)
        total = total + exchanged(total, 0, 1 << k)
        total = total + exchanged(total, 2, 4 if k == 2 else 0)
        old = (own, other)
        own, other = total, exchanged(total, 1, 0)
        if turn < ITERS - 1:
            sums, product = local_call(own_kernel, "own", (old[0], own, both), (square, small))
            sums, mine = local_call(other_kernel, "other", (old[1], other, sums, product, both), (square, small))
            scale = (local_call(scale_kernel, "scale", (*scale, sums), square, (1 << 10, 1 << 14)),)
    big = jax.ShapeDtypeStruct((1, 1, rows, cols), BF16)
    return pl.pallas_call(
        last_kernel,
        out_shape=(big, big, jax.ShapeDtypeStruct((1, 1, rank, cols), F32)),
        in_specs=[VMEM] * 9,
        out_specs=(HBM,) * 3,
        scratch_shapes=[
            pltpu.VMEM((rows, cols), BF16),
            pltpu.VMEM((rows, cols), BF16),
            pltpu.VMEM((rank, cols), F32),
            pltpu.SemaphoreType.DMA((2, 2, half // CHUNK)),
            pltpu.SemaphoreType.DMA,
        ],
        compiler_params=pltpu.CompilerParams(vmem_limit_bytes=LIMIT),
        name="last",
    )(*scale, *old, own, other, left, start, local, moment)


def on_device(global_params, local_params, momentum, init_factors, seeds, plan, round_index):
    start, local, moment = global_params[0, 0], local_params[0, 0], momentum[0, 0]
    rows, cols = start.shape
    rank = init_factors.shape[2]
    narrow = jax.ShapeDtypeStruct((rank, cols // 2), F32)
    both = pl.pallas_call(
        split_kernel,
        out_shape=jax.ShapeDtypeStruct((2 * rows, cols), BF16),
        in_specs=[ANY] * 2,
        out_specs=VMEM,
        scratch_shapes=[
            pltpu.VMEM((rows, cols), BF16),
            pltpu.VMEM((rows, cols), BF16),
            pltpu.SemaphoreType.DMA((2, cols // PART)),
        ],
        compiler_params=pltpu.CompilerParams(vmem_limit_bytes=LIMIT),
        cost_estimate=pl.CostEstimate(flops=1 << 21, bytes_accessed=1 << 23, transcendentals=0),
        name="split",
    )(start, local)
    level, own, other, mine = pl.pallas_call(
        first_kernel,
        out_shape=(jax.ShapeDtypeStruct((1,), jnp.int32), narrow, narrow, jax.ShapeDtypeStruct((rank, rows), F32)),
        in_specs=[SMEM] * 3 + [VMEM] * 2,
        out_specs=(SMEM,) + (VMEM,) * 3,
        compiler_params=pltpu.CompilerParams(vmem_limit_bytes=LIMIT),
        name="first",
    )(seeds, plan, round_index.reshape(1), init_factors, both)
    branches = [functools.partial(branch, k) for k in range(3)]
    return lax.switch(level[0], branches, own, other, both, mine, start, local, moment)


def solution(mesh):
    return jax.shard_map(
        on_device,
        mesh=mesh,
        in_specs=(
            P("island", None, "fsdp", None),
            P("island", None, "fsdp", None),
            P("island", None, "fsdp", None),
            P(),
            P(),
            P(),
            P(),
        ),
        out_specs=(
            P("island", None, "fsdp", None),
            P("island", None, "fsdp", None),
            P("island", None, None, None),
        ),
        check_vma=False,
    )
```

```python
import functools

import jax
import jax.numpy as jnp
from jax import lax
from jax.experimental import pallas as pl
from jax.experimental.pallas import tpu as pltpu
from jax.sharding import PartitionSpec as P

ITERS = 3
F32 = jnp.float32
BF16 = jnp.bfloat16
VMEM = pl.BlockSpec(memory_space=pltpu.VMEM)
SMEM = pl.BlockSpec(memory_space=pltpu.SMEM)
HBM = pl.BlockSpec(memory_space=pltpu.HBM)
ANY = pl.BlockSpec(memory_space=pl.ANY)
CHUNK = 512
PART = 1024
LANES = 128
LIMIT = 24 << 20
FULL = 55 << 20


def split3(x):
    high = x.astype(BF16).astype(F32)
    rest = x - high
    middle = rest.astype(BF16).astype(F32)
    return high, middle, rest - middle


def stacked(x):
    return jnp.concatenate(split3(x), axis=0).astype(BF16)


def unstacked(x):
    rank = x.shape[0] // 3
    return x[0:rank] + x[rank : 2 * rank] + x[2 * rank : 3 * rank]


def columns(start, width):
    return pl.ds(pl.multiple_of(start, width), width)


def left_product(factor, both):
    return lax.dot_general(stacked(factor), both, (((1,), (1,)), ((), ())), preferred_element_type=F32)


def folded(acc):
    rows = acc.shape[1] // 2
    total = unstacked(acc)
    return total[:, :rows] + total[:, rows:]


def core_side(flip):
    core = lax.rem(lax.axis_index("fsdp"), 2)
    return 1 - core if flip else core


def split_kernel(start_hbm, local_hbm, near, far, start, local, sems):
    rows, cols = start.shape
    half = cols // 2
    parts = half // PART

    sides = (core_side(False), core_side(True))

    def loads(n, j):
        s = columns(sides[n] * half + j * PART, PART)
        return s, (
            pltpu.make_async_copy(start_hbm.at[:, s], start.at[:, s], sems.at[0, n, j]),
            pltpu.make_async_copy(local_hbm.at[:, s], local.at[:, s], sems.at[1, n, j]),
        )

    for j in range(parts):
        for n in range(2):
            for copy in loads(n, j)[1]:
                copy.start()

    def step(j, carry):
        t = columns(j * PART, PART)
        for n, out in enumerate((near, far)):
            s, copies = loads(n, j)
            for copy in copies:
                copy.wait()
            delta = start[:, s].astype(F32) - local[:, s].astype(F32)
            high = delta.astype(BF16)
            out[0:rows, t] = high
            out[rows : 2 * rows, t] = (delta - high.astype(F32)).astype(BF16)
        return carry

    lax.fori_loop(0, parts, step, 0)


def first_kernel(seeds, plan, turn, init, near, far, level, own, other, left, scale):
    row = lax.broadcasted_iota(jnp.int32, scale.shape, 0)
    scale[...] = jnp.where(row == lax.broadcasted_iota(jnp.int32, scale.shape, 1), 1.0, 0.0)
    offset = plan[lax.rem(turn[0], plan.shape[0])]
    island = lax.axis_index("island")
    chosen = seeds[jnp.minimum(island, jnp.bitwise_xor(island, offset))]
    level[0] = lax.shift_right_logical(offset, 1)
    rank, half = own.shape
    own[...] = init[chosen, 0, :, columns(core_side(False) * half, half)]
    other[...] = init[chosen, 0, :, columns(core_side(True) * half, half)]

    def step(j, acc):
        s = columns(j * CHUNK, CHUNK)
        return acc + left_product(own[:, s], near[:, s]) + left_product(other[:, s], far[:, s])

    acc = jnp.zeros((3 * rank, near.shape[0]), F32)
    left[...] = folded(lax.fori_loop(0, half // CHUNK, step, acc))


def difference(scale, mine, peer):
    diff = mine[...] - peer[...]
    total = scale[0] * diff[0:1, :]
    for k in range(1, diff.shape[0]):
        total = total + scale[k] * diff[k : k + 1, :]
    return total


def right_half(left, pieces, out):
    lhs = stacked(left)
    lhs = jnp.concatenate([lhs, lhs], axis=1)

    def step(j, carry):
        s = columns(j * CHUNK, CHUNK)
        out[:, s] = unstacked(jnp.dot(lhs, pieces[:, s], preferred_element_type=F32))
        return carry

    lax.fori_loop(0, out.shape[1] // CHUNK, step, 0, unroll=2)


def give_kernel(scale, mine, peer, far, give, left):
    left[...] = difference(scale, mine, peer)
    right_half(left[...], far, give)


def keep_kernel(left, near, keep, kept):
    kept[...] = left[...]
    right_half(left[...], near, keep)


def pair_sums(old, new):
    rank, half = new.shape

    def step(j, accs):
        s = columns(j * CHUNK, CHUNK)
        q = old[:, s]
        u = new[:, s]
        return tuple(acc + q * u[k : k + 1, :] for k, acc in enumerate(accs))

    accs = lax.fori_loop(0, half // CHUNK, step, (jnp.zeros((rank, CHUNK), F32),) * rank)
    out = []
    for acc in accs:
        total = acc[:, 0:LANES]
        for n in range(1, CHUNK // LANES):
            total = total + acc[:, n * LANES : (n + 1) * LANES]
        out.append(total)
    return out


def left_half(new, pieces):
    rank, half = new.shape

    def step(j, acc):
        s = columns(j * CHUNK, CHUNK)
        return acc + left_product(new[:, s], pieces[:, s])

    return folded(lax.fori_loop(0, half // CHUNK, step, jnp.zeros((3 * rank, pieces.shape[0]), F32), unroll=2))


def own_kernel(old, new, near, sums, product):
    for k, total in enumerate(pair_sums(old, new)):
        sums[k] = total
    product[...] = left_half(new, near)


def other_kernel(old, new, own_sums, own_product, far, sums, product):
    for k, total in enumerate(pair_sums(old, new)):
        sums[k] = own_sums[k] + total
    product[...] = own_product[...] + left_half(new, far)


def inverse_columns(scale, sums):
    rank = len(sums)
    gram = []
    for j in range(rank):
        dots = jnp.sum(sums[j], axis=1, keepdims=True) + jnp.zeros((rank, LANES), F32)
        total = scale[0] * dots[0:1, :]
        for k in range(1, rank):
            total = total + scale[k] * dots[k : k + 1, :]
        gram.append(total)
    g = [[gram[j][i : i + 1, :] for j in range(rank)] for i in range(rank)]
    lower = [[None] * rank for _ in range(rank)]
    inv = [[None] * rank for _ in range(rank)]
    for j in range(rank):
        d = g[j][j]
        for k in range(j):
            d = d - lower[j][k] * lower[j][k]
        inv[j][j] = 1.0 / jnp.sqrt(d)
        for i in range(j + 1, rank):
            s = g[i][j]
            for k in range(j):
                s = s - lower[i][k] * lower[j][k]
            lower[i][j] = s * inv[j][j]
    for j in range(rank):
        for i in range(j + 1, rank):
            s = lower[i][j] * inv[j][j]
            for k in range(j + 1, i):
                s = s + lower[i][k] * inv[k][j]
            inv[i][j] = -s * inv[i][i]
    row = lax.broadcasted_iota(jnp.int32, (rank, LANES), 0)
    cols = []
    for j in range(rank):
        col = jnp.zeros((rank, LANES), F32)
        for i in range(j, rank):
            col = jnp.where(row == i, inv[i][j], col)
        cols.append(col)
    return cols


def scale_kernel(scale, sums, out, kept):
    for k, col in enumerate(inverse_columns(scale, [sums[k] for k in range(sums.shape[0])])):
        out[k] = col
        kept[k] = col


def last_kernel(scale, old_own, old_other, own, other, left, start_hbm, local_hbm, momentum_hbm, params_hbm, moved_hbm, factor_hbm, start, local, momentum, params, moved, factor, in_sems, sems, factor_sem):
    rank, half = own.shape
    parts = half // CHUNK
    sides = (core_side(False), core_side(True))
    loads = ((start_hbm, start), (local_hbm, local), (momentum_hbm, momentum))

    def fetches(j, n, t):
        return [pltpu.make_async_copy(src.at[:, t], dst.at[:, t], in_sems.at[m, n, j]) for m, (src, dst) in enumerate(loads)]

    for j in range(parts):
        for n, side in enumerate(sides):
            for copy in fetches(j, n, columns(side * half + j * CHUNK, CHUNK)):
                copy.start()
    sums = [a + b for a, b in zip(pair_sums(old_own, own), pair_sums(old_other, other))]
    inv = inverse_columns(scale, sums)
    wide = [jnp.concatenate([col] * (CHUNK // LANES), axis=1) for col in inv]

    def solved(by, u):
        total = by[0] * u[0:1, :]
        for k in range(1, rank):
            total = total + by[k] * u[k : k + 1, :]
        return total

    def sends(j, n, t):
        return (
            pltpu.make_async_copy(moved.at[:, t], moved_hbm.at[0, 0, :, t], sems.at[0, n, j]),
            pltpu.make_async_copy(params.at[:, t], params_hbm.at[0, 0, :, t], sems.at[1, n, j]),
        )

    b1, b2, b3 = split3(solved(inv, left[...]))
    basis = jnp.concatenate([b1, b1, b2, b2, b1, b3], axis=0).T.astype(BF16)

    def step(j, carry):
        s = columns(j * CHUNK, CHUNK)
        for n, (part, side) in enumerate(zip((own, other), sides)):
            t = columns(side * half + j * CHUNK, CHUNK)
            q = solved(wide, part[:, s])
            factor[:, t] = q
            q1, q2, q3 = split3(q)
            rhs = jnp.concatenate([q1, q2, q1, q2, q3, q1], axis=0).astype(BF16)
            correction = jnp.dot(basis, rhs, preferred_element_type=F32)
            for copy in fetches(j, n, t):
                copy.wait()
            base = start[:, t].astype(F32)
            gossiped = (base - local[:, t].astype(F32)) - 0.5 * correction
            velocity = 0.9 * momentum[:, t].astype(F32) + gossiped
            moved[:, t] = velocity.astype(BF16)
            params[:, t] = (base - 0.7 * (gossiped + 0.9 * velocity)).astype(BF16)
            for copy in sends(j, n, t):
                copy.start()
        return carry

    lax.fori_loop(0, parts, step, 0)
    sent = pltpu.make_async_copy(factor, factor_hbm.at[0, 0], factor_sem)
    sent.start()

    def drain(j, carry):
        for n, side in enumerate(sides):
            for copy in sends(j, n, columns(side * half + j * CHUNK, CHUNK)):
                copy.wait()
        return carry

    lax.fori_loop(0, parts, drain, 0)
    sent.wait()


def exchanged(x, fsdp_mask, island_mask):
    n_island, n_fsdp = lax.axis_size("island"), lax.axis_size("fsdp")
    if island_mask == 0:
        return lax.ppermute(x, "fsdp", [(i, i ^ fsdp_mask) for i in range(n_fsdp)])
    if fsdp_mask == 0:
        return lax.ppermute(x, "island", [(i, i ^ island_mask) for i in range(n_island)])
    pairs = []
    for i in range(n_island):
        for f in range(n_fsdp):
            pairs.append((i * n_fsdp + f, (i ^ island_mask) * n_fsdp + (f ^ fsdp_mask)))
    return lax.ppermute(x, ("island", "fsdp"), pairs)


def local_call(kernel, name, inputs, out_shape, cost=(1 << 20, 1 << 20)):
    return pl.pallas_call(
        kernel,
        out_shape=out_shape,
        in_specs=[VMEM] * len(inputs),
        out_specs=jax.tree.map(lambda _: VMEM, out_shape),
        compiler_params=pltpu.CompilerParams(vmem_limit_bytes=LIMIT),
        cost_estimate=pl.CostEstimate(flops=cost[0], bytes_accessed=cost[1], transcendentals=0),
        name=name,
    )(*inputs)


def head(k, scale, mine, near, far):
    narrow = jax.ShapeDtypeStruct((mine.shape[0], near.shape[1]), F32)
    peer = exchanged(mine, 0, 1 << k)
    small = jax.ShapeDtypeStruct(mine.shape, F32)
    give, left = local_call(give_kernel, "give", (scale, mine, peer, far), (narrow, small))
    keep, left = local_call(keep_kernel, "keep", (left, near), (narrow, small))
    total = keep + exchanged(give, 1, 0)
    return lax.optimization_barrier((left, total + exchanged(total, 0, 1 << k)))


def tail(total, level):
    for mask in (4, 8, 24):
        total = total + exchanged(total, mask, 0)
    return total + exchanged(total, 2, 4 if level == 2 else 0)


def middle(own, other, total, near, far, mine, scale):
    small = jax.ShapeDtypeStruct(mine.shape, F32)
    square = jax.ShapeDtypeStruct(scale.shape, F32)
    rest = exchanged(total, 1, 0)
    sums, product = local_call(own_kernel, "own", (own, total, near), (square, small))
    sums, mine = local_call(other_kernel, "other", (other, rest, sums, product, far), (square, small))
    scale, kept = local_call(scale_kernel, "scale", (scale, sums), (square, square), (1 << 10, 1 << 14))
    return total, rest, mine, scale, kept


def later(k, own, other, near, far, mine, scale):
    left, total = head(k, scale, mine, near, far)
    own, other, mine, scale, kept = middle(own, other, tail(total, k), near, far, mine, scale)
    left, total = head(k, scale, mine, near, far)
    return lax.optimization_barrier((kept, own, other, left, total))


def on_device(global_params, local_params, momentum, init_factors, seeds, plan, round_index):
    start, local, moment = global_params[0, 0], local_params[0, 0], momentum[0, 0]
    rows, cols = start.shape
    rank = init_factors.shape[2]
    narrow = jax.ShapeDtypeStruct((rank, cols // 2), F32)
    near, far = pl.pallas_call(
        split_kernel,
        out_shape=(jax.ShapeDtypeStruct((2 * rows, cols // 2), BF16),) * 2,
        in_specs=[ANY] * 2,
        out_specs=(VMEM,) * 2,
        scratch_shapes=[
            pltpu.VMEM((rows, cols), BF16),
            pltpu.VMEM((rows, cols), BF16),
            pltpu.SemaphoreType.DMA((2, 2, cols // 2 // PART)),
        ],
        compiler_params=pltpu.CompilerParams(vmem_limit_bytes=FULL),
        cost_estimate=pl.CostEstimate(flops=1 << 21, bytes_accessed=1 << 23, transcendentals=0),
        name="split",
    )(start, local)
    level, own, other, mine, scale = pl.pallas_call(
        first_kernel,
        out_shape=(jax.ShapeDtypeStruct((1,), jnp.int32), narrow, narrow, jax.ShapeDtypeStruct((rank, rows), F32), jax.ShapeDtypeStruct((rank, rank, LANES), F32)),
        in_specs=[SMEM] * 3 + [VMEM] * 3,
        out_specs=(SMEM,) + (VMEM,) * 4,
        compiler_params=pltpu.CompilerParams(vmem_limit_bytes=LIMIT),
        name="first",
    )(seeds, plan, round_index.reshape(1), init_factors, near, far)
    heads = [functools.partial(head, k) for k in range(3)]
    _, total = lax.switch(level[0], heads, scale, mine, near, far)
    own, other, mine, scale, _ = middle(own, other, tail(total, None), near, far, mine, scale)
    laters = [functools.partial(later, k) for k in range(3)]
    scale, own, other, left, total = lax.switch(level[0], laters, own, other, near, far, mine, scale)
    total = tail(total, None)
    rest = exchanged(total, 1, 0)
    big = jax.ShapeDtypeStruct((1, 1, rows, cols), BF16)
    return pl.pallas_call(
        last_kernel,
        out_shape=(big, big, jax.ShapeDtypeStruct((1, 1, rank, cols), F32)),
        in_specs=[VMEM] * 6 + [ANY] * 3,
        out_specs=(HBM,) * 3,
        scratch_shapes=[
            pltpu.VMEM((rows, cols), BF16),
            pltpu.VMEM((rows, cols), BF16),
            pltpu.VMEM((rows, cols), BF16),
            pltpu.VMEM((rows, cols), BF16),
            pltpu.VMEM((rows, cols), BF16),
            pltpu.VMEM((rank, cols), F32),
            pltpu.SemaphoreType.DMA((3, 2, cols // 2 // CHUNK)),
            pltpu.SemaphoreType.DMA((2, 2, cols // 2 // CHUNK)),
            pltpu.SemaphoreType.DMA,
        ],
        compiler_params=pltpu.CompilerParams(vmem_limit_bytes=52 << 20),
        name="last",
    )(scale, own, other, total, rest, left, start, local, moment)


def solution(mesh):
    return jax.shard_map(
        on_device,
        mesh=mesh,
        in_specs=(
            P("island", None, "fsdp", None),
            P("island", None, "fsdp", None),
            P("island", None, "fsdp", None),
            P(),
            P(),
            P(),
            P(),
        ),
        out_specs=(
            P("island", None, "fsdp", None),
            P("island", None, "fsdp", None),
            P("island", None, None, None),
        ),
        check_vma=False,
    )
```

```python
import functools

import jax
import jax.numpy as jnp
from jax import lax
from jax.experimental import pallas as pl
from jax.experimental.pallas import tpu as pltpu
from jax.sharding import PartitionSpec as P

ITERS = 3
F32 = jnp.float32
BF16 = jnp.bfloat16
VMEM = pl.BlockSpec(memory_space=pltpu.VMEM)
SMEM = pl.BlockSpec(memory_space=pltpu.SMEM)
HBM = pl.BlockSpec(memory_space=pltpu.HBM)
ANY = pl.BlockSpec(memory_space=pl.ANY)
CHUNK = 512
PART = 1024
LANES = 128
LIMIT = 24 << 20
FULL = 55 << 20


def split3(x):
    high = x.astype(BF16).astype(F32)
    rest = x - high
    middle = rest.astype(BF16).astype(F32)
    return high, middle, rest - middle


def stacked(x):
    return jnp.concatenate(split3(x), axis=0).astype(BF16)


def unstacked(x):
    rank = x.shape[0] // 3
    return x[0:rank] + x[rank : 2 * rank] + x[2 * rank : 3 * rank]


def columns(start, width):
    return pl.ds(pl.multiple_of(start, width), width)


def left_product(factor, both):
    return lax.dot_general(stacked(factor), both, (((1,), (1,)), ((), ())), preferred_element_type=F32)


def folded(acc):
    rows = acc.shape[1] // 2
    total = unstacked(acc)
    return total[:, :rows] + total[:, rows:]


def core_side(flip):
    core = lax.rem(lax.axis_index("fsdp"), 2)
    return 1 - core if flip else core


def split_kernel(start_hbm, local_hbm, near, far, start, local, sems):
    rows, cols = start.shape
    half = cols // 2
    parts = half // PART

    sides = (core_side(False), core_side(True))

    def loads(n, j):
        s = columns(sides[n] * half + j * PART, PART)
        return s, (
            pltpu.make_async_copy(start_hbm.at[:, s], start.at[:, s], sems.at[0, n, j]),
            pltpu.make_async_copy(local_hbm.at[:, s], local.at[:, s], sems.at[1, n, j]),
        )

    for j in range(parts):
        for n in range(2):
            for copy in loads(n, j)[1]:
                copy.start()

    def step(j, carry):
        t = columns(j * PART, PART)
        for n, out in enumerate((near, far)):
            s, copies = loads(n, j)
            for copy in copies:
                copy.wait()
            delta = start[:, s].astype(F32) - local[:, s].astype(F32)
            high = delta.astype(BF16)
            out[0:rows, t] = high
            out[rows : 2 * rows, t] = (delta - high.astype(F32)).astype(BF16)
        return carry

    lax.fori_loop(0, parts, step, 0)


def first_kernel(seeds, plan, turn, init, near, far, level, own, other, left, scale):
    row = lax.broadcasted_iota(jnp.int32, scale.shape, 0)
    scale[...] = jnp.where(row == lax.broadcasted_iota(jnp.int32, scale.shape, 1), 1.0, 0.0)
    offset = plan[lax.rem(turn[0], plan.shape[0])]
    island = lax.axis_index("island")
    chosen = seeds[jnp.minimum(island, jnp.bitwise_xor(island, offset))]
    level[0] = lax.shift_right_logical(offset, 1)
    rank, half = own.shape
    own[...] = init[chosen, 0, :, columns(core_side(False) * half, half)]
    other[...] = init[chosen, 0, :, columns(core_side(True) * half, half)]

    def step(j, acc):
        s = columns(j * CHUNK, CHUNK)
        return acc + left_product(own[:, s], near[:, s]) + left_product(other[:, s], far[:, s])

    acc = jnp.zeros((3 * rank, near.shape[0]), F32)
    left[...] = folded(lax.fori_loop(0, half // CHUNK, step, acc))


def difference(scale, mine, peer):
    diff = mine[...] - peer[...]
    total = scale[0] * diff[0:1, :]
    for k in range(1, diff.shape[0]):
        total = total + scale[k] * diff[k : k + 1, :]
    return total


def right_half(left, pieces, out):
    lhs = stacked(left)
    lhs = jnp.concatenate([lhs, lhs], axis=1)

    def step(j, carry):
        s = columns(j * CHUNK, CHUNK)
        out[:, s] = unstacked(jnp.dot(lhs, pieces[:, s], preferred_element_type=F32))
        return carry

    lax.fori_loop(0, out.shape[1] // CHUNK, step, 0, unroll=2)


def give_kernel(scale, mine, peer, far, give, left):
    left[...] = difference(scale, mine, peer)
    right_half(left[...], far, give)


def keep_kernel(left, near, keep, kept):
    kept[...] = left[...]
    right_half(left[...], near, keep)


def pair_sums(old, new):
    rank, half = new.shape

    def step(j, accs):
        s = columns(j * CHUNK, CHUNK)
        q = old[:, s]
        u = new[:, s]
        return tuple(acc + q * u[k : k + 1, :] for k, acc in enumerate(accs))

    accs = lax.fori_loop(0, half // CHUNK, step, (jnp.zeros((rank, CHUNK), F32),) * rank)
    out = []
    for acc in accs:
        total = acc[:, 0:LANES]
        for n in range(1, CHUNK // LANES):
            total = total + acc[:, n * LANES : (n + 1) * LANES]
        out.append(total)
    return out


def left_half(new, pieces):
    rank, half = new.shape

    def step(j, acc):
        s = columns(j * CHUNK, CHUNK)
        return acc + left_product(new[:, s], pieces[:, s])

    return folded(lax.fori_loop(0, half // CHUNK, step, jnp.zeros((3 * rank, pieces.shape[0]), F32), unroll=2))


def own_kernel(old, new, near, sums, product):
    for k, total in enumerate(pair_sums(old, new)):
        sums[k] = total
    product[...] = left_half(new, near)


def other_kernel(old, new, own_sums, own_product, far, sums, product):
    for k, total in enumerate(pair_sums(old, new)):
        sums[k] = own_sums[k] + total
    product[...] = own_product[...] + left_half(new, far)


def inverse_columns(scale, sums):
    rank = len(sums)
    gram = []
    for j in range(rank):
        dots = jnp.sum(sums[j], axis=1, keepdims=True) + jnp.zeros((rank, LANES), F32)
        total = scale[0] * dots[0:1, :]
        for k in range(1, rank):
            total = total + scale[k] * dots[k : k + 1, :]
        gram.append(total)
    g = [[gram[j][i : i + 1, :] for j in range(rank)] for i in range(rank)]
    lower = [[None] * rank for _ in range(rank)]
    inv = [[None] * rank for _ in range(rank)]
    for j in range(rank):
        d = g[j][j]
        for k in range(j):
            d = d - lower[j][k] * lower[j][k]
        inv[j][j] = 1.0 / jnp.sqrt(d)
        for i in range(j + 1, rank):
            s = g[i][j]
            for k in range(j):
                s = s - lower[i][k] * lower[j][k]
            lower[i][j] = s * inv[j][j]
    for j in range(rank):
        for i in range(j + 1, rank):
            s = lower[i][j] * inv[j][j]
            for k in range(j + 1, i):
                s = s + lower[i][k] * inv[k][j]
            inv[i][j] = -s * inv[i][i]
    row = lax.broadcasted_iota(jnp.int32, (rank, LANES), 0)
    cols = []
    for j in range(rank):
        col = jnp.zeros((rank, LANES), F32)
        for i in range(j, rank):
            col = jnp.where(row == i, inv[i][j], col)
        cols.append(col)
    return cols


def scale_kernel(scale, sums, out, kept):
    for k, col in enumerate(inverse_columns(scale, [sums[k] for k in range(sums.shape[0])])):
        out[k] = col
        kept[k] = col


def sums_kernel(old, new, sums):
    for k, total in enumerate(pair_sums(old, new)):
        sums[k] = total


def base_kernel(flip, start_hbm, local_hbm, momentum_hbm, moved, params, start, local, momentum, sems):
    half = moved.shape[1]
    parts = half // PART
    offset = core_side(flip) * half
    loads = ((start_hbm, start), (local_hbm, local), (momentum_hbm, momentum))

    def fetches(j):
        t = columns(offset + j * PART, PART)
        s = columns(j * PART, PART)
        return [pltpu.make_async_copy(src.at[:, t], dst.at[:, s], sems.at[m, j]) for m, (src, dst) in enumerate(loads)]

    for j in range(parts):
        for copy in fetches(j):
            copy.start()

    def step(j, carry):
        for copy in fetches(j):
            copy.wait()
        s = columns(j * PART, PART)
        base = start[:, s].astype(F32)
        delta = base - local[:, s].astype(F32)
        velocity = 0.9 * momentum[:, s].astype(F32) + delta
        moved[:, s] = velocity
        params[:, s] = base - 0.7 * (delta + 0.9 * velocity)
        return carry

    lax.fori_loop(0, parts, step, 0)


def last_kernel(scale, own_sums, old, own, other, left, own_moved, own_params, other_moved, other_params, params_hbm, moved_hbm, factor_hbm, params, moved, factor, sems, factor_sem):
    rank, half = own.shape
    parts = half // CHUNK
    sides = (core_side(False), core_side(True))
    sums = [own_sums[k] + total for k, total in enumerate(pair_sums(old, other))]
    inv = inverse_columns(scale, sums)
    wide = [jnp.concatenate([col] * (CHUNK // LANES), axis=1) for col in inv]

    def solved(by, u):
        total = by[0] * u[0:1, :]
        for k in range(1, rank):
            total = total + by[k] * u[k : k + 1, :]
        return total

    def sends(j, n, t):
        return (
            pltpu.make_async_copy(moved.at[:, t], moved_hbm.at[0, 0, :, t], sems.at[0, n, j]),
            pltpu.make_async_copy(params.at[:, t], params_hbm.at[0, 0, :, t], sems.at[1, n, j]),
        )

    b1, b2, b3 = split3(solved(inv, left[...]))
    basis = jnp.concatenate([b1, b1, b2, b2, b1, b3], axis=0).T.astype(BF16)
    halves = ((own, own_moved, own_params), (other, other_moved, other_params))

    def step(j, carry):
        s = columns(j * CHUNK, CHUNK)
        for n, (part, moved_base, params_base) in enumerate(halves):
            t = columns(sides[n] * half + j * CHUNK, CHUNK)
            q = solved(wide, part[:, s])
            factor[:, t] = q
            q1, q2, q3 = split3(q)
            rhs = jnp.concatenate([q1, q2, q1, q2, q3, q1], axis=0).astype(BF16)
            correction = jnp.dot(basis, rhs, preferred_element_type=F32)
            moved[:, t] = (moved_base[:, s] - 0.5 * correction).astype(BF16)
            params[:, t] = (params_base[:, s] + (0.7 * 0.5 * 1.9) * correction).astype(BF16)
            for copy in sends(j, n, t):
                copy.start()
        return carry

    lax.fori_loop(0, parts, step, 0)
    sent = pltpu.make_async_copy(factor, factor_hbm.at[0, 0], factor_sem)
    sent.start()

    def drain(j, carry):
        for n in range(2):
            for copy in sends(j, n, columns(sides[n] * half + j * CHUNK, CHUNK)):
                copy.wait()
        return carry

    lax.fori_loop(0, parts, drain, 0)
    sent.wait()


def exchanged(x, fsdp_mask, island_mask):
    n_island, n_fsdp = lax.axis_size("island"), lax.axis_size("fsdp")
    if island_mask == 0:
        return lax.ppermute(x, "fsdp", [(i, i ^ fsdp_mask) for i in range(n_fsdp)])
    if fsdp_mask == 0:
        return lax.ppermute(x, "island", [(i, i ^ island_mask) for i in range(n_island)])
    pairs = []
    for i in range(n_island):
        for f in range(n_fsdp):
            pairs.append((i * n_fsdp + f, (i ^ island_mask) * n_fsdp + (f ^ fsdp_mask)))
    return lax.ppermute(x, ("island", "fsdp"), pairs)


def local_call(kernel, name, inputs, out_shape, cost=(1 << 20, 1 << 20)):
    return pl.pallas_call(
        kernel,
        out_shape=out_shape,
        in_specs=[VMEM] * len(inputs),
        out_specs=jax.tree.map(lambda _: VMEM, out_shape),
        compiler_params=pltpu.CompilerParams(vmem_limit_bytes=LIMIT),
        cost_estimate=pl.CostEstimate(flops=cost[0], bytes_accessed=cost[1], transcendentals=0),
        name=name,
    )(*inputs)


def base_call(flip, start, local, moment, limit):
    rows, cols = start.shape
    half = cols // 2
    return pl.pallas_call(
        functools.partial(base_kernel, flip),
        out_shape=(jax.ShapeDtypeStruct((rows, half), F32),) * 2,
        in_specs=[ANY] * 3,
        out_specs=(VMEM,) * 2,
        scratch_shapes=[pltpu.VMEM((rows, half), BF16)] * 3 + [pltpu.SemaphoreType.DMA((3, half // PART))],
        compiler_params=pltpu.CompilerParams(vmem_limit_bytes=limit),
        cost_estimate=pl.CostEstimate(flops=1 << 22, bytes_accessed=1 << 22, transcendentals=0),
        name="base",
    )(start, local, moment)


def head(k, scale, mine, near, far):
    narrow = jax.ShapeDtypeStruct((mine.shape[0], near.shape[1]), F32)
    peer = exchanged(mine, 0, 1 << k)
    small = jax.ShapeDtypeStruct(mine.shape, F32)
    give, left = local_call(give_kernel, "give", (scale, mine, peer, far), (narrow, small))
    keep, left = local_call(keep_kernel, "keep", (left, near), (narrow, small))
    total = keep + exchanged(give, 1, 0)
    return lax.optimization_barrier((left, total + exchanged(total, 0, 1 << k)))


def tail(total, level):
    for mask in (4, 8, 24):
        total = total + exchanged(total, mask, 0)
    return total + exchanged(total, 2, 4 if level == 2 else 0)


def middle(own, other, total, near, far, mine, scale):
    small = jax.ShapeDtypeStruct(mine.shape, F32)
    square = jax.ShapeDtypeStruct(scale.shape, F32)
    rest = exchanged(total, 1, 0)
    sums, product = local_call(own_kernel, "own", (own, total, near), (square, small))
    sums, mine = local_call(other_kernel, "other", (other, rest, sums, product, far), (square, small))
    scale, kept = local_call(scale_kernel, "scale", (scale, sums), (square, square), (1 << 10, 1 << 14))
    return total, rest, mine, scale, kept


def later(k, own, other, near, far, mine, scale):
    left, total = head(k, scale, mine, near, far)
    own, other, mine, scale, kept = middle(own, other, tail(total, k), near, far, mine, scale)
    left, total = head(k, scale, mine, near, far)
    return lax.optimization_barrier((kept, own, other, left, total))


def on_device(global_params, local_params, momentum, init_factors, seeds, plan, round_index):
    start, local, moment = global_params[0, 0], local_params[0, 0], momentum[0, 0]
    rows, cols = start.shape
    rank = init_factors.shape[2]
    narrow = jax.ShapeDtypeStruct((rank, cols // 2), F32)
    near, far = pl.pallas_call(
        split_kernel,
        out_shape=(jax.ShapeDtypeStruct((2 * rows, cols // 2), BF16),) * 2,
        in_specs=[ANY] * 2,
        out_specs=(VMEM,) * 2,
        scratch_shapes=[
            pltpu.VMEM((rows, cols), BF16),
            pltpu.VMEM((rows, cols), BF16),
            pltpu.SemaphoreType.DMA((2, 2, cols // 2 // PART)),
        ],
        compiler_params=pltpu.CompilerParams(vmem_limit_bytes=FULL),
        cost_estimate=pl.CostEstimate(flops=1 << 21, bytes_accessed=1 << 23, transcendentals=0),
        name="split",
    )(start, local)
    level, own, other, mine, scale = pl.pallas_call(
        first_kernel,
        out_shape=(jax.ShapeDtypeStruct((1,), jnp.int32), narrow, narrow, jax.ShapeDtypeStruct((rank, rows), F32), jax.ShapeDtypeStruct((rank, rank, LANES), F32)),
        in_specs=[SMEM] * 3 + [VMEM] * 3,
        out_specs=(SMEM,) + (VMEM,) * 4,
        compiler_params=pltpu.CompilerParams(vmem_limit_bytes=LIMIT),
        name="first",
    )(seeds, plan, round_index.reshape(1), init_factors, near, far)
    heads = [functools.partial(head, k) for k in range(3)]
    _, total = lax.switch(level[0], heads, scale, mine, near, far)
    own, other, mine, scale, _ = middle(own, other, tail(total, None), near, far, mine, scale)
    laters = [functools.partial(later, k) for k in range(3)]
    scale, own, other, left, total = lax.switch(level[0], laters, own, other, near, far, mine, scale)
    bases = []
    for n, mask in enumerate((4, 8, 24)):
        moved = exchanged(total, mask, 0)
        if n < 2:
            total, start, local, moment = lax.optimization_barrier((total, start, local, moment))
            part = base_call(n == 1, start, local, moment, (48, 44)[n] << 20)
            moved, *part = lax.optimization_barrier((moved, *part))
            bases += part
        total = total + moved
    total = total + exchanged(total, 2, 0)
    rest = exchanged(total, 1, 0)
    sums = local_call(sums_kernel, "sums", (own, total), jax.ShapeDtypeStruct(scale.shape, F32))
    big = jax.ShapeDtypeStruct((1, 1, rows, cols), BF16)
    return pl.pallas_call(
        last_kernel,
        out_shape=(big, big, jax.ShapeDtypeStruct((1, 1, rank, cols), F32)),
        in_specs=[VMEM] * 10,
        out_specs=(HBM,) * 3,
        scratch_shapes=[
            pltpu.VMEM((rows, cols), BF16),
            pltpu.VMEM((rows, cols), BF16),
            pltpu.VMEM((rank, cols), F32),
            pltpu.SemaphoreType.DMA((2, 2, cols // 2 // CHUNK)),
            pltpu.SemaphoreType.DMA,
        ],
        compiler_params=pltpu.CompilerParams(vmem_limit_bytes=LIMIT),
        name="last",
    )(scale, sums, other, total, rest, left, *bases)


def solution(mesh):
    return jax.shard_map(
        on_device,
        mesh=mesh,
        in_specs=(
            P("island", None, "fsdp", None),
            P("island", None, "fsdp", None),
            P("island", None, "fsdp", None),
            P(),
            P(),
            P(),
            P(),
        ),
        out_specs=(
            P("island", None, "fsdp", None),
            P("island", None, "fsdp", None),
            P("island", None, None, None),
        ),
        check_vma=False,
    )
```

```python
import functools

import jax
import jax.numpy as jnp
from jax import lax
from jax.experimental import pallas as pl
from jax.experimental.pallas import tpu as pltpu
from jax.sharding import PartitionSpec as P

ITERS = 3
F32 = jnp.float32
BF16 = jnp.bfloat16
VMEM = pl.BlockSpec(memory_space=pltpu.VMEM)
SMEM = pl.BlockSpec(memory_space=pltpu.SMEM)
HBM = pl.BlockSpec(memory_space=pltpu.HBM)
ANY = pl.BlockSpec(memory_space=pl.ANY)
CHUNK = 512
PART = 1024
LANES = 128
LIMIT = 24 << 20
FULL = 55 << 20


def split3(x):
    high = x.astype(BF16).astype(F32)
    rest = x - high
    middle = rest.astype(BF16).astype(F32)
    return high, middle, rest - middle


def stacked(x):
    return jnp.concatenate(split3(x), axis=0).astype(BF16)


def unstacked(x):
    rank = x.shape[0] // 3
    return x[0:rank] + x[rank : 2 * rank] + x[2 * rank : 3 * rank]


def columns(start, width):
    return pl.ds(pl.multiple_of(start, width), width)


def left_product(factor, both):
    return lax.dot_general(stacked(factor), both, (((1,), (1,)), ((), ())), preferred_element_type=F32)


def folded(acc):
    rows = acc.shape[1] // 2
    total = unstacked(acc)
    return total[:, :rows] + total[:, rows:]


def core_side(flip):
    core = lax.rem(lax.axis_index("fsdp"), 2)
    return 1 - core if flip else core


def split_kernel(start_hbm, local_hbm, near, far, start, local, sems):
    rows, cols = start.shape
    half = cols // 2
    parts = half // PART

    sides = (core_side(False), core_side(True))

    def loads(n, j):
        s = columns(sides[n] * half + j * PART, PART)
        return s, (
            pltpu.make_async_copy(start_hbm.at[:, s], start.at[:, s], sems.at[0, n, j]),
            pltpu.make_async_copy(local_hbm.at[:, s], local.at[:, s], sems.at[1, n, j]),
        )

    for j in range(parts):
        for n in range(2):
            for copy in loads(n, j)[1]:
                copy.start()

    def step(j, carry):
        t = columns(j * PART, PART)
        for n, out in enumerate((near, far)):
            s, copies = loads(n, j)
            for copy in copies:
                copy.wait()
            delta = start[:, s].astype(F32) - local[:, s].astype(F32)
            high = delta.astype(BF16)
            out[0:rows, t] = high
            out[rows : 2 * rows, t] = (delta - high.astype(F32)).astype(BF16)
        return carry

    lax.fori_loop(0, parts, step, 0)


def first_kernel(seeds, plan, turn, init, near, far, level, own, other, left, scale):
    row = lax.broadcasted_iota(jnp.int32, scale.shape, 0)
    scale[...] = jnp.where(row == lax.broadcasted_iota(jnp.int32, scale.shape, 1), 1.0, 0.0)
    offset = plan[lax.rem(turn[0], plan.shape[0])]
    island = lax.axis_index("island")
    chosen = seeds[jnp.minimum(island, jnp.bitwise_xor(island, offset))]
    level[0] = lax.shift_right_logical(offset, 1)
    rank, half = own.shape
    own[...] = init[chosen, 0, :, columns(core_side(False) * half, half)]
    other[...] = init[chosen, 0, :, columns(core_side(True) * half, half)]

    def step(j, acc):
        s = columns(j * CHUNK, CHUNK)
        return acc + left_product(own[:, s], near[:, s]) + left_product(other[:, s], far[:, s])

    acc = jnp.zeros((3 * rank, near.shape[0]), F32)
    left[...] = folded(lax.fori_loop(0, half // CHUNK, step, acc))


def difference(scale, mine, peer):
    diff = mine[...] - peer[...]
    total = scale[0] * diff[0:1, :]
    for k in range(1, diff.shape[0]):
        total = total + scale[k] * diff[k : k + 1, :]
    return total


def right_half(left, pieces, out):
    lhs = stacked(left)
    lhs = jnp.concatenate([lhs, lhs], axis=1)

    def step(j, carry):
        s = columns(j * CHUNK, CHUNK)
        out[:, s] = unstacked(jnp.dot(lhs, pieces[:, s], preferred_element_type=F32))
        return carry

    lax.fori_loop(0, out.shape[1] // CHUNK, step, 0, unroll=4)


def give_kernel(scale, mine, peer, far, give, left):
    left[...] = difference(scale, mine, peer)
    right_half(left[...], far, give)


def keep_kernel(left, near, keep, kept):
    kept[...] = left[...]
    right_half(left[...], near, keep)


def pair_sums(old, new):
    rank, half = new.shape

    def step(j, accs):
        s = columns(j * CHUNK, CHUNK)
        q = old[:, s]
        u = new[:, s]
        return tuple(acc + q * u[k : k + 1, :] for k, acc in enumerate(accs))

    accs = lax.fori_loop(0, half // CHUNK, step, (jnp.zeros((rank, CHUNK), F32),) * rank, unroll=2)
    out = []
    for acc in accs:
        total = acc[:, 0:LANES]
        for n in range(1, CHUNK // LANES):
            total = total + acc[:, n * LANES : (n + 1) * LANES]
        out.append(total)
    return out


def left_half(new, pieces):
    rank, half = new.shape

    def step(j, acc):
        s = columns(j * CHUNK, CHUNK)
        return acc + left_product(new[:, s], pieces[:, s])

    return folded(lax.fori_loop(0, half // CHUNK, step, jnp.zeros((3 * rank, pieces.shape[0]), F32), unroll=4))


def own_kernel(old, new, near, sums, product):
    for k, total in enumerate(pair_sums(old, new)):
        sums[k] = total
    product[...] = left_half(new, near)


def other_kernel(old, new, own_sums, own_product, far, sums, product):
    for k, total in enumerate(pair_sums(old, new)):
        sums[k] = own_sums[k] + total
    product[...] = own_product[...] + left_half(new, far)


def inverse_columns(scale, sums):
    rank = len(sums)
    gram = []
    for j in range(rank):
        dots = jnp.sum(sums[j], axis=1, keepdims=True) + jnp.zeros((rank, LANES), F32)
        total = scale[0] * dots[0:1, :]
        for k in range(1, rank):
            total = total + scale[k] * dots[k : k + 1, :]
        gram.append(total)
    g = [[gram[j][i : i + 1, :] for j in range(rank)] for i in range(rank)]
    lower = [[None] * rank for _ in range(rank)]
    inv = [[None] * rank for _ in range(rank)]
    for j in range(rank):
        d = g[j][j]
        for k in range(j):
            d = d - lower[j][k] * lower[j][k]
        inv[j][j] = 1.0 / jnp.sqrt(d)
        for i in range(j + 1, rank):
            s = g[i][j]
            for k in range(j):
                s = s - lower[i][k] * lower[j][k]
            lower[i][j] = s * inv[j][j]
    for j in range(rank):
        for i in range(j + 1, rank):
            s = lower[i][j] * inv[j][j]
            for k in range(j + 1, i):
                s = s + lower[i][k] * inv[k][j]
            inv[i][j] = -s * inv[i][i]
    row = lax.broadcasted_iota(jnp.int32, (rank, LANES), 0)
    cols = []
    for j in range(rank):
        col = jnp.zeros((rank, LANES), F32)
        for i in range(j, rank):
            col = jnp.where(row == i, inv[i][j], col)
        cols.append(col)
    return cols


def scale_kernel(scale, sums, out, kept):
    for k, col in enumerate(inverse_columns(scale, [sums[k] for k in range(sums.shape[0])])):
        out[k] = col
        kept[k] = col


def sums_kernel(old, new, sums):
    for k, total in enumerate(pair_sums(old, new)):
        sums[k] = total


def base_kernel(flip, start_hbm, local_hbm, momentum_hbm, moved, params, start, local, momentum, sems):
    half = moved.shape[1]
    parts = half // PART
    offset = core_side(flip) * half
    loads = ((start_hbm, start), (local_hbm, local), (momentum_hbm, momentum))

    def fetches(j):
        t = columns(offset + j * PART, PART)
        s = columns(j * PART, PART)
        return [pltpu.make_async_copy(src.at[:, t], dst.at[:, s], sems.at[m, j]) for m, (src, dst) in enumerate(loads)]

    for j in range(parts):
        for copy in fetches(j):
            copy.start()

    def step(j, carry):
        for copy in fetches(j):
            copy.wait()
        s = columns(j * PART, PART)
        base = start[:, s].astype(F32)
        delta = base - local[:, s].astype(F32)
        velocity = 0.9 * momentum[:, s].astype(F32) + delta
        moved[:, s] = velocity
        params[:, s] = base - 0.7 * (delta + 0.9 * velocity)
        return carry

    lax.fori_loop(0, parts, step, 0)


def last_kernel(scale, own_sums, old, own, other, left, own_moved, own_params, other_moved, other_params, params_hbm, moved_hbm, factor_hbm, params, moved, factor, sems, factor_sem):
    rank, half = own.shape
    parts = half // CHUNK
    sides = (core_side(False), core_side(True))
    sums = [own_sums[k] + total for k, total in enumerate(pair_sums(old, other))]
    inv = inverse_columns(scale, sums)
    wide = [jnp.concatenate([col] * (CHUNK // LANES), axis=1) for col in inv]

    def solved(by, u):
        total = by[0] * u[0:1, :]
        for k in range(1, rank):
            total = total + by[k] * u[k : k + 1, :]
        return total

    def sends(j, n, t):
        return (
            pltpu.make_async_copy(moved.at[:, t], moved_hbm.at[0, 0, :, t], sems.at[0, n, j]),
            pltpu.make_async_copy(params.at[:, t], params_hbm.at[0, 0, :, t], sems.at[1, n, j]),
        )

    b1, b2, b3 = split3(solved(inv, left[...]))
    basis = jnp.concatenate([b1, b1, b2, b2, b1, b3], axis=0).T.astype(BF16)
    halves = ((own, own_moved, own_params), (other, other_moved, other_params))

    def step(j, carry):
        s = columns(j * CHUNK, CHUNK)
        for n, (part, moved_base, params_base) in enumerate(halves):
            t = columns(sides[n] * half + j * CHUNK, CHUNK)
            q = solved(wide, part[:, s])
            factor[:, t] = q
            q1, q2, q3 = split3(q)
            rhs = jnp.concatenate([q1, q2, q1, q2, q3, q1], axis=0).astype(BF16)
            correction = jnp.dot(basis, rhs, preferred_element_type=F32)
            moved[:, t] = (moved_base[:, s] - 0.5 * correction).astype(BF16)
            params[:, t] = (params_base[:, s] + (0.7 * 0.5 * 1.9) * correction).astype(BF16)
            for copy in sends(j, n, t):
                copy.start()
        return carry

    lax.fori_loop(0, parts, step, 0)
    sent = pltpu.make_async_copy(factor, factor_hbm.at[0, 0], factor_sem)
    sent.start()

    def drain(j, carry):
        for n in range(2):
            for copy in sends(j, n, columns(sides[n] * half + j * CHUNK, CHUNK)):
                copy.wait()
        return carry

    lax.fori_loop(0, parts, drain, 0)
    sent.wait()


def exchanged(x, fsdp_mask, island_mask):
    n_island, n_fsdp = lax.axis_size("island"), lax.axis_size("fsdp")
    if island_mask == 0:
        return lax.ppermute(x, "fsdp", [(i, i ^ fsdp_mask) for i in range(n_fsdp)])
    if fsdp_mask == 0:
        return lax.ppermute(x, "island", [(i, i ^ island_mask) for i in range(n_island)])
    pairs = []
    for i in range(n_island):
        for f in range(n_fsdp):
            pairs.append((i * n_fsdp + f, (i ^ island_mask) * n_fsdp + (f ^ fsdp_mask)))
    return lax.ppermute(x, ("island", "fsdp"), pairs)


def local_call(kernel, name, inputs, out_shape, cost=(1 << 20, 1 << 20)):
    return pl.pallas_call(
        kernel,
        out_shape=out_shape,
        in_specs=[VMEM] * len(inputs),
        out_specs=jax.tree.map(lambda _: VMEM, out_shape),
        compiler_params=pltpu.CompilerParams(vmem_limit_bytes=LIMIT),
        cost_estimate=pl.CostEstimate(flops=cost[0], bytes_accessed=cost[1], transcendentals=0),
        name=name,
    )(*inputs)


def base_call(flip, start, local, moment, limit):
    rows, cols = start.shape
    half = cols // 2
    return pl.pallas_call(
        functools.partial(base_kernel, flip),
        out_shape=(jax.ShapeDtypeStruct((rows, half), F32),) * 2,
        in_specs=[ANY] * 3,
        out_specs=(VMEM,) * 2,
        scratch_shapes=[pltpu.VMEM((rows, half), BF16)] * 3 + [pltpu.SemaphoreType.DMA((3, half // PART))],
        compiler_params=pltpu.CompilerParams(vmem_limit_bytes=limit),
        cost_estimate=pl.CostEstimate(flops=1 << 22, bytes_accessed=1 << 22, transcendentals=0),
        name="base",
    )(start, local, moment)


def head(k, scale, mine, near, far):
    narrow = jax.ShapeDtypeStruct((mine.shape[0], near.shape[1]), F32)
    peer = exchanged(mine, 0, 1 << k)
    small = jax.ShapeDtypeStruct(mine.shape, F32)
    give, left = local_call(give_kernel, "give", (scale, mine, peer, far), (narrow, small))
    keep, left = local_call(keep_kernel, "keep", (left, near), (narrow, small))
    total = keep + exchanged(give, 1, 0)
    return lax.optimization_barrier((left, total + exchanged(total, 0, 1 << k)))


def tail(total, level):
    for mask in (4, 8, 24):
        total = total + exchanged(total, mask, 0)
    return total + exchanged(total, 2, 4 if level == 2 else 0)


def middle(own, other, total, near, far, mine, scale):
    small = jax.ShapeDtypeStruct(mine.shape, F32)
    square = jax.ShapeDtypeStruct(scale.shape, F32)
    rest = exchanged(total, 1, 0)
    sums, product = local_call(own_kernel, "own", (own, total, near), (square, small))
    sums, mine = local_call(other_kernel, "other", (other, rest, sums, product, far), (square, small))
    scale, kept = local_call(scale_kernel, "scale", (scale, sums), (square, square), (1 << 10, 1 << 14))
    return total, rest, mine, scale, kept


def later(k, own, other, near, far, mine, scale):
    left, total = head(k, scale, mine, near, far)
    own, other, mine, scale, kept = middle(own, other, tail(total, k), near, far, mine, scale)
    left, total = head(k, scale, mine, near, far)
    return lax.optimization_barrier((kept, own, other, left, total))


def on_device(global_params, local_params, momentum, init_factors, seeds, plan, round_index):
    start, local, moment = global_params[0, 0], local_params[0, 0], momentum[0, 0]
    rows, cols = start.shape
    rank = init_factors.shape[2]
    narrow = jax.ShapeDtypeStruct((rank, cols // 2), F32)
    near, far = pl.pallas_call(
        split_kernel,
        out_shape=(jax.ShapeDtypeStruct((2 * rows, cols // 2), BF16),) * 2,
        in_specs=[ANY] * 2,
        out_specs=(VMEM,) * 2,
        scratch_shapes=[
            pltpu.VMEM((rows, cols), BF16),
            pltpu.VMEM((rows, cols), BF16),
            pltpu.SemaphoreType.DMA((2, 2, cols // 2 // PART)),
        ],
        compiler_params=pltpu.CompilerParams(vmem_limit_bytes=FULL),
        cost_estimate=pl.CostEstimate(flops=1 << 21, bytes_accessed=1 << 23, transcendentals=0),
        name="split",
    )(start, local)
    level, own, other, mine, scale = pl.pallas_call(
        first_kernel,
        out_shape=(jax.ShapeDtypeStruct((1,), jnp.int32), narrow, narrow, jax.ShapeDtypeStruct((rank, rows), F32), jax.ShapeDtypeStruct((rank, rank, LANES), F32)),
        in_specs=[SMEM] * 3 + [VMEM] * 3,
        out_specs=(SMEM,) + (VMEM,) * 4,
        compiler_params=pltpu.CompilerParams(vmem_limit_bytes=LIMIT),
        name="first",
    )(seeds, plan, round_index.reshape(1), init_factors, near, far)
    heads = [functools.partial(head, k) for k in range(3)]
    _, total = lax.switch(level[0], heads, scale, mine, near, far)
    own, other, mine, scale, _ = middle(own, other, tail(total, None), near, far, mine, scale)
    laters = [functools.partial(later, k) for k in range(3)]
    scale, own, other, left, total = lax.switch(level[0], laters, own, other, near, far, mine, scale)
    bases = []
    for n, mask in enumerate((4, 8, 24)):
        moved = exchanged(total, mask, 0)
        if n < 2:
            total, start, local, moment = lax.optimization_barrier((total, start, local, moment))
            part = base_call(n == 1, start, local, moment, (48, 44)[n] << 20)
            moved, *part = lax.optimization_barrier((moved, *part))
            bases += part
        total = total + moved
    total = total + exchanged(total, 2, 0)
    rest = exchanged(total, 1, 0)
    sums = local_call(sums_kernel, "sums", (own, total), jax.ShapeDtypeStruct(scale.shape, F32))
    big = jax.ShapeDtypeStruct((1, 1, rows, cols), BF16)
    return pl.pallas_call(
        last_kernel,
        out_shape=(big, big, jax.ShapeDtypeStruct((1, 1, rank, cols), F32)),
        in_specs=[VMEM] * 10,
        out_specs=(HBM,) * 3,
        scratch_shapes=[
            pltpu.VMEM((rows, cols), BF16),
            pltpu.VMEM((rows, cols), BF16),
            pltpu.VMEM((rank, cols), F32),
            pltpu.SemaphoreType.DMA((2, 2, cols // 2 // CHUNK)),
            pltpu.SemaphoreType.DMA,
        ],
        compiler_params=pltpu.CompilerParams(vmem_limit_bytes=LIMIT),
        name="last",
    )(scale, sums, other, total, rest, left, *bases)


def solution(mesh):
    return jax.shard_map(
        on_device,
        mesh=mesh,
        in_specs=(
            P("island", None, "fsdp", None),
            P("island", None, "fsdp", None),
            P("island", None, "fsdp", None),
            P(),
            P(),
            P(),
            P(),
        ),
        out_specs=(
            P("island", None, "fsdp", None),
            P("island", None, "fsdp", None),
            P("island", None, None, None),
        ),
        check_vma=False,
    )
```
